32 devices in a mesh: tile: 8 (over z, y), clip: 4 (over x, core).
Axes of the slice: x: 2, y: 2, z: 4, core: 2. Of those that a mesh axis runs over, the one named last changes fastest.
Arguments:
- seq_rows: bfloat16 [32768, 512], P(('tile', 'clip'))
- plan_owner: int32 [32768], P(('tile', 'clip')), may hold values from 0 to 31, as said below
- plan_slot: int32 [32768], P(('tile', 'clip')), may hold values from 0 to 1023, as said below
- live_frames: int32 [4], replicated, may hold values from 1 to 4, as said below
- norm_gain: float32 [512], replicated, may hold values from 0.1 to 1.9
- norm_bias: float32 [512], replicated, may hold values from -3 to 3
- conv_weight: bfloat16 [3, 3, 512, 3, 256], replicated, may hold values from -0.0546875 to 0.0546875
- conv_bias: float32 [256], replicated, may hold values from -3 to 3
Outputs:
- decoded: bfloat16 [4, 8, 4, 8, 32, 256], P('clip', 'tile')
The draws below stay inside these ranges and needn't reach their ends.
Inputs may be any that keep to these rules, and one draw needn't show every extreme that they name: `plan_owner`: owner o is tile o % 8 of clip o // 8. The 1024 rows of each device send 32 // 2 or 48 rows to each owner, so at most 48, which is reached. The pairs of plan_owner and plan_slot are all distinct: every slot of every owner receives exactly one row. `live_frames`: some clip has all 4 frames live.
All inputs are finite; a program needn't handle non-finite values.
Results may differ from the reference program's by a relative error of at most 0.004.
Values may be sent and summed in bfloat16 or wider, within the bound.
A program may use at most 128 MiB of HBM per device.

```python
import math
import jax
import jax.numpy as jnp
from jax import lax

C = 512
CO = 256
GROUPS = 32
LT = 4
TH = 8
TW = 32
GW = 4
TILES = 8
CLIPS = 4
OWNERS = 32
ROWS_DEV = 1024
PER = 32
SEQ = 32768


def plan_tables(key):
    base = jax.random.fold_in(key, 17)
    key_first, key_second, key_slots, key_order = jax.random.split(base, 4)
    first = jax.random.permutation(key_first, OWNERS)
    second = jax.random.permutation(key_second, OWNERS)
    pattern = (first[:, None] + second[None, :]) % OWNERS < OWNERS // 2
    counts = PER // 2 + PER * pattern.astype(jnp.int32)
    ends = jnp.cumsum(counts, axis=1)
    starts = ends - counts
    position = jnp.arange(ROWS_DEV, dtype=jnp.int32)
    owner_of = jax.vmap(lambda row_ends: jnp.searchsorted(row_ends, position, side='right'))(ends).astype(jnp.int32)
    ranking = position[None, :] - jnp.take_along_axis(starts, owner_of, axis=1)
    earlier = jnp.cumsum(counts, axis=0) - counts
    linear = jnp.take_along_axis(earlier, owner_of, axis=1) + ranking
    shuffles = jax.vmap(lambda single: jax.random.permutation(single, ROWS_DEV))(jax.random.split(key_slots, OWNERS)).astype(jnp.int32)
    slots = shuffles[owner_of, linear]
    orders = jax.vmap(lambda single: jax.random.permutation(single, ROWS_DEV))(jax.random.split(key_order, OWNERS)).astype(jnp.int32)
    owner_final = jnp.take_along_axis(owner_of, orders, axis=1)
    slot_final = jnp.take_along_axis(slots, orders, axis=1)
    return (owner_final.reshape(-1).astype(jnp.int32), slot_final.reshape(-1).astype(jnp.int32))


def draw_plan_owner(key, part):
    return plan_tables(key)[0]


def draw_plan_slot(key, part):
    return plan_tables(key)[1]


def draw_live_frames(key, part):
    drawn = jax.random.randint(jax.random.fold_in(key, 3), (CLIPS,), 1, LT + 1)
    chosen = jax.random.randint(jax.random.fold_in(key, 5), (), 0, CLIPS)
    return jnp.where(jnp.arange(CLIPS) == chosen, LT, drawn).astype(jnp.int32)


def draw_seq_rows(key, part):
    owners, slots = plan_tables(key)
    tile_of = (owners % TILES).astype(jnp.float32)
    key_noise, key_scale = jax.random.split(jax.random.fold_in(key, 29), 2)
    ramp = tile_of / max(TILES - 1, 1)
    noise = jnp.clip(jax.random.normal(key_noise, (SEQ, C)), -6.0, 6.0)
    channel_scale = jnp.exp(jax.random.uniform(key_scale, (C,)) * math.log(10.0))
    row_scale = 1.0 + 2.0 * ramp
    values = noise * channel_scale[None, :] * row_scale[:, None]
    return values.astype(jnp.float32).astype(jnp.bfloat16)


def gaussian(stream_key, shape, scale, bound, kind=jnp.bfloat16):
    values = scale * jax.random.normal(stream_key, shape, jnp.float32)
    return jnp.clip(values, min=-bound, max=bound).astype(kind)


def setup_inputs(seed: int = 0) -> dict:
    splits = jax.random.split(jax.random.key(seed), 9)
    return {
        "seq_rows": draw_seq_rows(jax.random.fold_in(splits[8], 71), 0),
        "plan_owner": draw_plan_owner(jax.random.fold_in(splits[8], 71), 0),
        "plan_slot": draw_plan_slot(jax.random.fold_in(splits[8], 71), 0),
        "live_frames": draw_live_frames(jax.random.fold_in(splits[8], 71), 0),
        "norm_gain": jnp.clip(1.0 + 0.18 * jax.random.normal(splits[4], (C,), jnp.float32), 0.1, 1.9),
        "norm_bias": gaussian(splits[5], (C,), 0.5, 3.0, jnp.float32),
        "conv_weight": gaussian(splits[6], (3, 3, C, 3, CO), (27 * C) ** -0.5, 0.0546875),
        "conv_bias": gaussian(splits[7], (CO,), 0.5, 3.0, jnp.float32),
    }


EPSILON = 1e-06

def reference(seq_rows, plan_owner, plan_slot, live_frames, norm_gain, norm_bias, conv_weight, conv_bias):
    channels = seq_rows.shape[1]
    out_width = conv_bias.shape[0]
    grid_rows = TILES // GW
    height = grid_rows * TH
    width_cells = GW * TW
    per_group = channels // GROUPS
    flat_index = (plan_owner * ROWS_DEV + plan_slot).astype(jnp.int32)
    placed = jnp.zeros((CLIPS * TILES * ROWS_DEV, channels), jnp.bfloat16).at[flat_index].set(seq_rows)
    placed = placed.reshape(CLIPS, grid_rows, GW, LT, TH, TW, channels)
    volume = placed.transpose(0, 3, 1, 4, 2, 5, 6).reshape(CLIPS, LT, height, width_cells, channels)
    kernel = conv_weight.astype(jnp.float32).transpose(0, 1, 3, 2, 4)

    def one_clip(item):
        clip_volume, frames = item
        values = clip_volume.astype(jnp.float32)
        live_frame = jnp.arange(LT) < frames
        live_weight = live_frame.astype(jnp.float32)[:, None, None, None]
        first_sum = lax.optimization_barrier(jnp.sum(values * live_weight, axis=(0, 1, 2))).reshape(GROUPS, per_group).sum(axis=1)
        second_sum = lax.optimization_barrier(jnp.sum(values * values * live_weight, axis=(0, 1, 2))).reshape(GROUPS, per_group).sum(axis=1)
        count_clip = per_group * frames.astype(jnp.float32) * (height * width_cells)
        mean_group = first_sum / count_clip
        scale_group = lax.rsqrt(second_sum / count_clip - mean_group * mean_group + EPSILON)
        mean_channel = jnp.repeat(mean_group, per_group)
        scale_channel = jnp.repeat(scale_group, per_group)
        normed = (values - mean_channel) * scale_channel * norm_gain + norm_bias
        activation = jax.nn.silu(normed).astype(jnp.bfloat16)
        mixed = lax.conv_general_dilated(activation.astype(jnp.float32)[None], kernel, (1, 1, 1), ((2, 0), (1, 1), (1, 1)), dimension_numbers=('NDHWC', 'DHWIO', 'NDHWC'), precision=lax.Precision.HIGHEST)[0]
        mixed = jnp.where(live_frame[:, None, None, None], mixed + conv_bias, 0.0)
        return mixed.astype(jnp.bfloat16)
    results = lax.map(one_clip, (volume, live_frames))
    results = results.reshape(CLIPS, LT, grid_rows, TH, GW, TW, out_width)
    results = results.transpose(0, 2, 4, 1, 3, 5, 6)
    return results.reshape(CLIPS, TILES, LT, TH, TW, out_width)
```

```python
import functools

import jax
import jax.numpy as jnp
from jax import lax
from jax.experimental import pallas as pl
from jax.experimental.pallas import tpu as pltpu
from jax.sharding import PartitionSpec as P

GROUPS = 32
LT = 4
TH = 8
TW = 32
GW = 4
PLANE = TH * TW
LANES = 128
STAT = 64
EPSILON = 1e-06
HIGHEST = lax.Precision.HIGHEST
F32 = jnp.float32
BF16 = jnp.bfloat16
NT = (((1,), (1,)), ((), ()))
MESH = pl.DeviceIdType.MESH
EDGES = ((0, 1), (0, -1), (1, 0), (-1, 0), (1, 1), (1, -1), (-1, 1), (-1, -1))


def iota(shape, axis):
    return lax.broadcasted_iota(jnp.int32, shape, axis)


def bits(n):
    return n.bit_length() - 1


def dot(a, b, **kw):
    return jnp.dot(a, b, preferred_element_type=F32, **kw)


def route_kernel(
    tiles,
    clips,
    cap,
    live_ref,
    owner_ref,
    slot_ref,
    rows_ref,
    x_ref,
    cols_ref,
    faces_ref,
    corners_ref,
    stats_ref,
    send_rows,
    recv_rows,
    send_meta,
    recv_meta,
    total,
    edge_out,
    face_out,
    edge_in,
    face_in,
    row_sent,
    row_got,
    meta_sent,
    meta_got,
    halo_sent,
    halo_got,
):
    count = tiles * clips
    half = tiles // 2
    own = count // 2
    rows, channels = rows_ref.shape
    my_tile = lax.axis_index("tile")
    my_clip = lax.axis_index("clip")
    my_half = my_tile // half
    my_local = my_tile % half

    def partner(k):
        rest = k % own
        to_half = (my_half + 1 + k // own) % 2
        to_tile = to_half * half + (my_local + rest // clips) % half
        return to_tile, (my_clip + rest % clips) % clips

    for buffer in (edge_in, face_in):
        buffer[...] = jnp.zeros_like(buffer)
    barrier = pltpu.get_barrier_semaphore()

    @pl.loop(0, count)
    def _(k):
        @pl.when(k != own)
        def _():
            pl.semaphore_signal(barrier, inc=1, device_id=partner(k), device_id_type=MESH)

    owner = owner_ref[...]
    slot = slot_ref[...]
    table = (iota((count, rows), 0) == owner).astype(F32)
    before = (iota((rows, rows), 0) < iota((rows, rows), 1)).astype(F32).astype(BF16)
    rank = jnp.sum(dot(table.astype(BF16), before) * table, axis=0, keepdims=True)
    to_clip = owner >> bits(tiles)
    to_tile = owner & (tiles - 1)
    same = ((to_tile >> bits(half)) == my_half).astype(jnp.int32)
    turn = ((to_tile & (half - 1)) - my_local) & (half - 1)
    order = same * own + turn * clips + ((to_clip - my_clip) & (clips - 1))
    position = order * cap + rank.astype(jnp.int32)

    clip_row = iota((8, rows), 0)
    live_limit = jnp.zeros((8, rows), jnp.int32)
    for c in range(clips):
        live_limit = jnp.where(clip_row == c, live_ref[c] * PLANE, live_limit)
    mask = ((clip_row == to_clip) & (slot < live_limit)).astype(F32).astype(BF16)
    values = rows_ref[...]
    wide = values.astype(F32)
    square = wide * wide
    high = square.astype(BF16)
    low = (square - high.astype(F32)).astype(BF16)
    sum1 = dot(mask, values)
    sum2 = dot(mask, high) + dot(mask, low)
    per_group = bits(channels // GROUPS)
    group = iota((channels, LANES), 0) >> per_group
    lane = iota((channels, LANES), 1)
    partial = dot(sum1, (lane - STAT == group).astype(F32), precision=HIGHEST) + dot(
        sum2, (lane - STAT - GROUPS == group).astype(F32), precision=HIGHEST
    )

    digits_row = iota((8, rows), 0)
    digits = jnp.where(digits_row == 0, slot >> 5, jnp.where(digits_row == 1, slot & 31, 0))
    digits = digits.astype(F32).astype(BF16)

    batch = max(8, min(count, 512 // cap // 8 * 8))
    size = batch * cap
    segment = iota((batch, size), 0) * cap
    column = iota((batch, size), 1)
    inside = (column >= segment) & (column < segment + cap)
    piece = (iota((cap, LANES), 0) == iota((cap, LANES), 1)).astype(F32).astype(BF16)
    place = jnp.concatenate([piece] * batch, axis=0)
    goes = (my_clip + iota((batch, LANES), 0)) & (clips - 1)
    stats = jnp.zeros((batch, LANES), F32)
    for c in range(clips):
        stats = jnp.where(goes == c, partial[c : c + 1], stats)

    def row_copy(k):
        return pltpu.make_async_remote_copy(
            src_ref=send_rows.at[k],
            dst_ref=recv_rows.at[k],
            send_sem=row_sent.at[k],
            recv_sem=row_got.at[k],
            device_id=partner(k),
            device_id_type=MESH,
        )

    def meta_copy(k):
        return pltpu.make_async_remote_copy(
            src_ref=send_meta.at[k],
            dst_ref=recv_meta.at[k],
            send_sem=meta_sent.at[k],
            recv_sem=meta_got.at[k],
            device_id=partner(k),
            device_id_type=MESH,
        )

    for step in range(count // batch):
        first = step * batch
        chosen = (iota((size, rows), 0) + first * cap == position).astype(F32).astype(BF16)
        packed = dot(chosen, values).astype(BF16)
        send_rows[first : first + batch] = packed.reshape(batch, cap, channels)
        slots = lax.dot_general(digits, chosen, NT, preferred_element_type=F32)
        upper = jnp.where(inside, slots[0:1], 0.0).astype(BF16)
        lower = jnp.where(inside, slots[1:2], 0.0).astype(BF16)
        meta = dot(upper, place) * 32.0 + dot(lower, place) + stats
        for i in range(batch):
            send_meta[first + i] = meta[i : i + 1]
        if first <= own < first + batch:
            recv_rows[own] = send_rows[own]
            recv_meta[own] = send_meta[own]
        if step == 0:
            pl.semaphore_wait(barrier, count - 1)

        @pl.loop(first, first + batch)
        def _(k):
            @pl.when(k != own)
            def _():
                meta_copy(k).start()
                row_copy(k).start()

    joint = max(1, min(count, 256 // cap))
    while count % joint:
        joint -= 1
    width = joint * cap
    spread_lane = iota((LANES, width), 0)
    spread_col = iota((LANES, width), 1)
    spread = jnp.zeros((LANES, width), F32)
    owner_of = jnp.zeros((8, width), jnp.int32)
    for m in range(joint):
        hit = (spread_col - m * cap == spread_lane) & (spread_lane < cap)
        spread = jnp.where(hit, 1.0, spread)
        owner_of = jnp.where(iota((8, width), 1) >= m * cap, m, owner_of)
    voxel = iota((rows, width), 0)
    sums_in = jnp.zeros((1, LANES), F32)
    depth = (joint + 7) // 8
    for step in range(count // joint):
        first = step * joint

        @pl.loop(first, first + joint)
        def _(k):
            @pl.when(k != own)
            def _():
                meta_copy(k).wait_recv()
                row_copy(k).wait_recv()

        slot_row = jnp.zeros((1, width), F32)
        for d in range(depth):
            metas = jnp.zeros((8, LANES), F32)
            for m in range(d * 8, min(joint, d * 8 + 8)):
                one = recv_meta[first + m]
                sums_in = sums_in + one
                metas = jnp.where(iota((8, LANES), 0) == m - d * 8, one, metas)
            moved = dot(metas, spread, precision=HIGHEST)
            keep = owner_of == iota((8, width), 0) + d * 8
            slot_row = slot_row + jnp.sum(jnp.where(keep, moved, 0.0), axis=0, keepdims=True)
        target = (voxel == (slot_row + 0.5).astype(jnp.int32)).astype(F32).astype(BF16)
        arrived = recv_rows[first : first + joint].reshape(width, channels)
        placed = dot(target, arrived)
        if step == 0:
            total[...] = placed
        else:
            total[...] += placed
    stats_ref[...] = sums_in

    tile = total[...].astype(BF16)
    grid = tile.reshape(LT, TH, TW, channels)
    x_ref[...] = grid
    face_out[0] = grid[:, TH - 1].reshape(LT * TW, channels)
    face_out[1] = grid[:, 0].reshape(LT * TW, channels)
    line = iota((128, rows), 0)
    source = iota((128, rows), 1)
    wanted = jnp.where(
        line < 32,
        line * TW + TW - 1,
        jnp.where(line < 64, (line - 32) * TW, -1),
    )
    for e, (down, right) in enumerate(EDGES[4:]):
        base = 64 + e * 16
        offset = (TH - 1 if down > 0 else 0) * TW + (TW - 1 if right > 0 else 0)
        in_corner = (line >= base) & (line < base + LT)
        wanted = jnp.where(in_corner, (line - base) * PLANE + offset, wanted)
    edges = dot((source == wanted).astype(F32).astype(BF16), tile).astype(BF16)
    edge_out[...] = edges

    grid_rows = tiles // GW
    row_tile = my_tile // GW
    column_tile = my_tile % GW

    def exists(down, right):
        row = row_tile + down
        column = column_tile + right
        return (row >= 0) & (row < grid_rows) & (column >= 0) & (column < GW)

    def halo_copy(e):
        down, right = EDGES[e]
        if e < 2:
            part, source_ref, target_ref = pl.ds(e * 32, 32), edge_out, edge_in
        elif e < 4:
            part, source_ref, target_ref = e - 2, face_out, face_in
        else:
            part, source_ref, target_ref = pl.ds(64 + (e - 4) * 16, 16), edge_out, edge_in
        return pltpu.make_async_remote_copy(
            src_ref=source_ref.at[part],
            dst_ref=target_ref.at[part],
            send_sem=halo_sent.at[e],
            recv_sem=halo_got.at[e],
            device_id=(my_tile + down * GW + right, my_clip),
            device_id_type=MESH,
        )

    for e in (2, 3, 0, 1, 4, 5, 6, 7):
        @pl.when(exists(*EDGES[e]))
        def _():
            halo_copy(e).start()

    @pl.loop(0, count)
    def _(k):
        @pl.when(k != own)
        def _():
            meta_copy(k).wait_send()
            row_copy(k).wait_send()

    for e, (down, right) in enumerate(EDGES):
        @pl.when(exists(-down, -right))
        def _():
            halo_copy(e).wait_recv()

    cols_ref[...] = edge_in[0:64]
    corners_ref[...] = edge_in[64:128]
    faces_ref[...] = face_in[...]
    for e, (down, right) in enumerate(EDGES):
        @pl.when(exists(down, right))
        def _():
            halo_copy(e).wait_send()


def conv_kernel(
    tiles,
    info_ref,
    x_ref,
    cols_ref,
    faces_ref,
    corners_ref,
    stats_ref,
    gain_ref,
    bias_ref,
    out_bias_ref,
    weight_ref,
    out_ref,
    padded,
    summed,
    edge_act,
):
    tap = pl.program_id(0)
    channels = x_ref.shape[-1]
    live = info_ref[0]

    @pl.when(tap == 0)
    def _():
        per_group = channels // GROUPS
        voxels = jnp.full((8, LANES), live * (per_group * PLANE * tiles), jnp.int32)
        scaled = stats_ref[...] / voxels.astype(F32)
        lane = iota((LANES, channels), 0)
        group = iota((LANES, channels), 1) >> bits(per_group)
        mean = dot(scaled, (lane - STAT == group).astype(F32), precision=HIGHEST)
        second = dot(scaled, (lane - STAT - GROUPS == group).astype(F32), precision=HIGHEST)
        scale = lax.rsqrt(second - mean * mean + EPSILON)
        scale = (scale * gain_ref[...])[0:1]
        mean = mean[0:1]
        bias = bias_ref[...]

        def activate(raw):
            v = (raw.astype(F32) - mean) * scale + bias
            return v / (1.0 + jnp.exp(-v))

        up, down = info_ref[1] > 0, info_ref[2] > 0
        left, right = info_ref[3] > 0, info_ref[4] > 0
        zero = jnp.zeros((1, channels), F32)
        edge_act[0:32] = jnp.where(left, activate(cols_ref[0:32]), zero)
        edge_act[32:64] = jnp.where(right, activate(cols_ref[32:64]), zero)
        for e, ok in enumerate((up & left, up & right, down & left, down & right)):
            edge_act[64 + e * 16 : 80 + e * 16] = jnp.where(
                ok, activate(corners_ref[e * 16 : e * 16 + 16]), zero
            )
        where = iota((TW, channels), 0)

        def put(t, h, y, left_row, right_row):
            before = jnp.where(where == 0, left_row, pltpu.roll(y, 1, 0))
            after = jnp.where(where == TW - 1, right_row, pltpu.roll(y, TW - 1, 0))
            padded[t, h, :, 0:channels] = before.astype(BF16)
            padded[t, h, :, channels : 2 * channels] = y.astype(BF16)
            padded[t, h, :, 2 * channels : 3 * channels] = after.astype(BF16)

        @pl.loop(0, LT * TH)
        def _(r):
            t, h = r // TH, r % TH
            put(
                t,
                h + 1,
                activate(x_ref[t, h]),
                edge_act[pl.ds(r, 1)],
                edge_act[pl.ds(r + 32, 1)],
            )

        for side, ok in enumerate((up, down)):
            for t in range(LT):
                y = jnp.where(ok, activate(faces_ref[side, t * TW : (t + 1) * TW]), zero)
                base = 64 + side * 32 + t
                put(
                    t,
                    side * (TH + 1),
                    y,
                    edge_act[base : base + 1],
                    edge_act[base + 16 : base + 17],
                )
        summed[...] = jnp.zeros_like(summed)

    weight = weight_ref[0]
    for a in range(3):
        @pl.when(tap // 3 == a)
        def _():
            frames = LT - 2 + a
            slab = padded[0:frames, pl.ds(tap % 3, TH)].reshape(frames * PLANE, 3 * channels)
            start = (2 - a) * PLANE
            summed[start:, :] += dot(slab, weight)

    @pl.when(tap == 8)
    def _():
        frame = iota(summed.shape, 0) >> bits(PLANE)
        decoded = jnp.where(frame < live, summed[...] + out_bias_ref[...], 0.0)
        out_ref[...] = decoded.astype(BF16)


def on_device(
    seq_rows, plan_owner, plan_slot, live_frames, norm_gain, norm_bias, conv_weight, conv_bias
):
    rows, channels = seq_rows.shape
    out_width = conv_bias.shape[0]
    tiles = lax.axis_size("tile")
    clips = lax.axis_size("clip")
    count = tiles * clips
    cap = -(-(3 * (rows // count) // 2) // 16) * 16
    vmem = pl.BlockSpec(memory_space=pltpu.VMEM)
    smem = pl.BlockSpec(memory_space=pltpu.SMEM)
    dma = pltpu.SemaphoreType.DMA
    x, cols, faces, corners, stats = pl.pallas_call(
        functools.partial(route_kernel, tiles, clips, cap),
        out_shape=(
            jax.ShapeDtypeStruct((LT, TH, TW, channels), BF16),
            jax.ShapeDtypeStruct((64, channels), BF16),
            jax.ShapeDtypeStruct((2, LT * TW, channels), BF16),
            jax.ShapeDtypeStruct((64, channels), BF16),
            jax.ShapeDtypeStruct((1, LANES), F32),
        ),
        in_specs=[smem, vmem, vmem, vmem],
        out_specs=(vmem,) * 5,
        scratch_shapes=[
            pltpu.VMEM((count, cap, channels), BF16),
            pltpu.VMEM((count, cap, channels), BF16),
            pltpu.VMEM((count, 1, LANES), F32),
            pltpu.VMEM((count, 1, LANES), F32),
            pltpu.VMEM((rows, channels), F32),
            pltpu.VMEM((128, channels), BF16),
            pltpu.VMEM((2, LT * TW, channels), BF16),
            pltpu.VMEM((128, channels), BF16),
            pltpu.VMEM((2, LT * TW, channels), BF16),
            dma((count,)),
            dma((count,)),
            dma((count,)),
            dma((count,)),
            dma((8,)),
            dma((8,)),
        ],
        compiler_params=pltpu.CompilerParams(
            collective_id=0, has_side_effects=True, vmem_limit_bytes=48 << 20
        ),
        name="route",
    )(live_frames, plan_owner.reshape(1, rows), plan_slot.reshape(1, rows), seq_rows)

    my_tile = lax.axis_index("tile")
    row_tile, column_tile = my_tile // GW, my_tile % GW
    info = jnp.stack(
        [
            live_frames[lax.axis_index("clip")],
            (row_tile > 0).astype(jnp.int32),
            (row_tile < tiles // GW - 1).astype(jnp.int32),
            (column_tile > 0).astype(jnp.int32),
            (column_tile < GW - 1).astype(jnp.int32),
        ]
    )
    weight = conv_weight.transpose(0, 1, 3, 2, 4).reshape(9, 3 * channels, out_width)

    def whole(*shape):
        return pl.BlockSpec(shape, lambda i: (0,) * len(shape))

    decoded = pl.pallas_call(
        functools.partial(conv_kernel, tiles),
        grid=(9,),
        out_shape=jax.ShapeDtypeStruct((rows, out_width), BF16),
        in_specs=[
            smem,
            whole(LT, TH, TW, channels),
            whole(64, channels),
            whole(2, LT * TW, channels),
            whole(64, channels),
            whole(1, LANES),
            whole(1, channels),
            whole(1, channels),
            whole(1, out_width),
            pl.BlockSpec((1, 3 * channels, out_width), lambda i: (i, 0, 0)),
        ],
        out_specs=whole(rows, out_width),
        scratch_shapes=[
            pltpu.VMEM((LT, TH + 2, TW, 3 * channels), BF16),
            pltpu.VMEM((rows, out_width), F32),
            pltpu.VMEM((128, channels), F32),
        ],
        compiler_params=pltpu.CompilerParams(
            dimension_semantics=("arbitrary",), vmem_limit_bytes=32 << 20
        ),
        name="convolve",
    )(
        info,
        x,
        cols,
        faces,
        corners,
        stats,
        norm_gain.reshape(1, channels),
        norm_bias.reshape(1, channels),
        conv_bias.reshape(1, out_width),
        weight,
    )
    return decoded.reshape(1, 1, LT, TH, TW, out_width)


def solution(mesh):
    return jax.shard_map(
        on_device,
        mesh=mesh,
        in_specs=(
            P(("tile", "clip"), None),
            P(("tile", "clip")),
            P(("tile", "clip")),
            P(),
            P(),
            P(),
            P(),
            P(),
        ),
        out_specs=P("clip", "tile", None, None, None, None),
        check_vma=False,
    )
```

```python
import functools

import jax
import jax.numpy as jnp
from jax import lax
from jax.experimental import pallas as pl
from jax.experimental.pallas import tpu as pltpu
from jax.sharding import PartitionSpec as P

GROUPS = 32
LT = 4
TH = 8
TW = 32
GW = 4
PLANE = TH * TW
LANES = 128
STAT = 64
EPSILON = 1e-06
HIGHEST = lax.Precision.HIGHEST
F32 = jnp.float32
BF16 = jnp.bfloat16
NT = (((1,), (1,)), ((), ()))
MESH = pl.DeviceIdType.MESH
EDGES = ((0, 1), (0, -1), (1, 0), (-1, 0), (1, 1), (1, -1), (-1, 1), (-1, -1))


def iota(shape, axis):
    return lax.broadcasted_iota(jnp.int32, shape, axis)


def bits(n):
    return n.bit_length() - 1


def dot(a, b, **kw):
    return jnp.dot(a, b, preferred_element_type=F32, **kw)


def decode_kernel(
    tiles,
    clips,
    cap,
    live_hbm,
    owner_hbm,
    slot_hbm,
    rows_hbm,
    gain_hbm,
    bias_hbm,
    out_bias_hbm,
    weight_hbm,
    out_ref,
    live_ref,
    owner_ref,
    slot_ref,
    rows_ref,
    gain_ref,
    bias_ref,
    out_bias_ref,
    weight_ref,
    send_rows,
    recv_rows,
    send_meta,
    recv_meta,
    total,
    edge_out,
    face_out,
    edge_in,
    face_in,
    padded,
    summed,
    edge_act,
    loaded,
    row_sent,
    row_got,
    meta_sent,
    meta_got,
    halo_sent,
    halo_got,
):
    loads = [
        pltpu.make_async_copy(source, target, loaded.at[i])
        for i, (source, target) in enumerate(
            (
                (owner_hbm, owner_ref),
                (slot_hbm, slot_ref),
                (live_hbm, live_ref),
                (rows_hbm, rows_ref),
                (gain_hbm, gain_ref),
                (bias_hbm, bias_ref),
                (out_bias_hbm, out_bias_ref),
                (weight_hbm, weight_ref),
            )
        )
    ]
    for load in loads:
        load.start()
    count = tiles * clips
    half = tiles // 2
    own = 1
    rows, channels = rows_ref.shape
    my_tile = lax.axis_index("tile")
    my_clip = lax.axis_index("clip")
    my_half = my_tile // half
    my_local = my_tile % half

    def partner(k):
        rest = k // 2
        to_half = (my_half + 1 + k % 2) % 2
        to_tile = to_half * half + (my_local + rest // clips) % half
        return to_tile, (my_clip + rest % clips) % clips

    for buffer in (edge_in, face_in):
        buffer[...] = jnp.zeros_like(buffer)
    barrier = pltpu.get_barrier_semaphore()

    @pl.loop(0, count)
    def _(k):
        @pl.when(k != own)
        def _():
            pl.semaphore_signal(barrier, inc=1, device_id=partner(k), device_id_type=MESH)

    for load in loads[:4]:
        load.wait()
    owner = owner_ref[...]
    slot = slot_ref[...]
    table = (iota((count, rows), 0) == owner).astype(F32)
    before = (iota((rows, rows), 0) < iota((rows, rows), 1)).astype(F32).astype(BF16)
    rank = jnp.sum(dot(table.astype(BF16), before) * table, axis=0, keepdims=True)
    to_clip = owner >> bits(tiles)
    to_tile = owner & (tiles - 1)
    same = ((to_tile >> bits(half)) == my_half).astype(jnp.int32)
    turn = ((to_tile & (half - 1)) - my_local) & (half - 1)
    order = 2 * (turn * clips + ((to_clip - my_clip) & (clips - 1))) + same
    position = order * cap + rank.astype(jnp.int32)

    clip_row = iota((8, rows), 0)
    live_limit = jnp.zeros((8, rows), jnp.int32)
    for c in range(clips):
        live_limit = jnp.where(clip_row == c, live_ref[c] * PLANE, live_limit)
    mask = ((clip_row == to_clip) & (slot < live_limit)).astype(F32).astype(BF16)
    values = rows_ref[...]
    wide = values.astype(F32)
    square = wide * wide
    high = square.astype(BF16)
    low = (square - high.astype(F32)).astype(BF16)
    sum1 = dot(mask, values)
    sum2 = dot(mask, high) + dot(mask, low)
    per_group = bits(channels // GROUPS)
    group = iota((channels, LANES), 0) >> per_group
    lane = iota((channels, LANES), 1)
    partial = dot(sum1, (lane - STAT == group).astype(F32), precision=HIGHEST) + dot(
        sum2, (lane - STAT - GROUPS == group).astype(F32), precision=HIGHEST
    )

    digits_row = iota((8, rows), 0)
    digits = jnp.where(digits_row == 0, slot >> 5, jnp.where(digits_row == 1, slot & 31, 0))
    digits = digits.astype(F32).astype(BF16)

    batch = max(2 * clips, min(count, 512 // cap // 8 * 8))
    size = batch * cap
    segment = iota((batch, size), 0) * cap
    column = iota((batch, size), 1)
    inside = (column >= segment) & (column < segment + cap)
    piece = (iota((cap, LANES), 0) == iota((cap, LANES), 1)).astype(F32).astype(BF16)
    place = jnp.concatenate([piece] * batch, axis=0)
    goes = (my_clip + (iota((batch, LANES), 0) >> 1)) & (clips - 1)
    stats = jnp.zeros((batch, LANES), F32)
    for c in range(clips):
        stats = jnp.where(goes == c, partial[c : c + 1], stats)

    def row_copy(k):
        return pltpu.make_async_remote_copy(
            src_ref=send_rows.at[k],
            dst_ref=recv_rows.at[k],
            send_sem=row_sent.at[k],
            recv_sem=row_got.at[k],
            device_id=partner(k),
            device_id_type=MESH,
        )

    def meta_copy(k):
        return pltpu.make_async_remote_copy(
            src_ref=send_meta.at[k],
            dst_ref=recv_meta.at[k],
            send_sem=meta_sent.at[k],
            recv_sem=meta_got.at[k],
            device_id=partner(k),
            device_id_type=MESH,
        )

    for step in range(count // batch):
        first = step * batch
        chosen = (iota((size, rows), 0) + first * cap == position).astype(F32).astype(BF16)
        packed = dot(chosen, values).astype(BF16)
        send_rows[first : first + batch] = packed.reshape(batch, cap, channels)
        slots = lax.dot_general(digits, chosen, NT, preferred_element_type=F32)
        upper = jnp.where(inside, slots[0:1], 0.0).astype(BF16)
        lower = jnp.where(inside, slots[1:2], 0.0).astype(BF16)
        meta = dot(upper, place) * 32.0 + dot(lower, place) + stats
        for i in range(batch):
            send_meta[first + i] = meta[i : i + 1]
        if first <= own < first + batch:
            recv_rows[own] = send_rows[own]
            recv_meta[own] = send_meta[own]
        if step == 0:
            pl.semaphore_wait(barrier, count - 1)

        @pl.loop(first, first + batch)
        def _(k):
            @pl.when(k != own)
            def _():
                meta_copy(k).start()
                row_copy(k).start()

    joint = max(1, min(count, 256 // cap))
    while count % joint:
        joint -= 1
    width = joint * cap
    spread_lane = iota((LANES, width), 0)
    spread_col = iota((LANES, width), 1)
    spread = jnp.zeros((LANES, width), F32)
    owner_of = jnp.zeros((8, width), jnp.int32)
    for m in range(joint):
        hit = (spread_col - m * cap == spread_lane) & (spread_lane < cap)
        spread = jnp.where(hit, 1.0, spread)
        owner_of = jnp.where(iota((8, width), 1) >= m * cap, m, owner_of)
    voxel = iota((rows, width), 0)
    sums_in = jnp.zeros((1, LANES), F32)
    depth = (joint + 7) // 8
    for step in range(count // joint):
        first = step * joint

        @pl.loop(first, first + joint)
        def _(k):
            @pl.when(k != own)
            def _():
                meta_copy(k).wait_recv()
                row_copy(k).wait_recv()

        slot_row = jnp.zeros((1, width), F32)
        for d in range(depth):
            metas = jnp.zeros((8, LANES), F32)
            for m in range(d * 8, min(joint, d * 8 + 8)):
                one = recv_meta[first + m]
                sums_in = sums_in + one
                metas = jnp.where(iota((8, LANES), 0) == m - d * 8, one, metas)
            moved = dot(metas, spread, precision=HIGHEST)
            keep = owner_of == iota((8, width), 0) + d * 8
            slot_row = slot_row + jnp.sum(jnp.where(keep, moved, 0.0), axis=0, keepdims=True)
        target = (voxel == (slot_row + 0.5).astype(jnp.int32)).astype(F32).astype(BF16)
        arrived = recv_rows[first : first + joint].reshape(width, channels)
        placed = dot(target, arrived)
        if step == 0:
            total[...] = placed
        else:
            total[...] += placed

    tile = total[...].astype(BF16)
    grid = tile.reshape(LT, TH, TW, channels)
    face_out[0] = grid[:, TH - 1].reshape(LT * TW, channels)
    face_out[1] = grid[:, 0].reshape(LT * TW, channels)
    line = iota((128, rows), 0)
    source = iota((128, rows), 1)
    wanted = jnp.where(
        line < 32,
        line * TW + TW - 1,
        jnp.where(line < 64, (line - 32) * TW, -1),
    )
    for e, (down, right) in enumerate(EDGES[4:]):
        base = 64 + e * 16
        offset = (TH - 1 if down > 0 else 0) * TW + (TW - 1 if right > 0 else 0)
        in_corner = (line >= base) & (line < base + LT)
        wanted = jnp.where(in_corner, (line - base) * PLANE + offset, wanted)
    edges = dot((source == wanted).astype(F32).astype(BF16), tile).astype(BF16)
    edge_out[...] = edges

    grid_rows = tiles // GW
    row_tile = my_tile // GW
    column_tile = my_tile % GW

    def exists(down, right):
        row = row_tile + down
        column = column_tile + right
        return (row >= 0) & (row < grid_rows) & (column >= 0) & (column < GW)

    def halo_copy(e):
        down, right = EDGES[e]
        if e < 2:
            part, source_ref, target_ref = pl.ds(e * 32, 32), edge_out, edge_in
        elif e < 4:
            part, source_ref, target_ref = e - 2, face_out, face_in
        else:
            part, source_ref, target_ref = pl.ds(64 + (e - 4) * 16, 16), edge_out, edge_in
        return pltpu.make_async_remote_copy(
            src_ref=source_ref.at[part],
            dst_ref=target_ref.at[part],
            send_sem=halo_sent.at[e],
            recv_sem=halo_got.at[e],
            device_id=(my_tile + down * GW + right, my_clip),
            device_id_type=MESH,
        )

    for e in (2, 3, 0, 1, 4, 5, 6, 7):
        @pl.when(exists(*EDGES[e]))
        def _():
            halo_copy(e).start()

    for load in loads[4:]:
        load.wait()
    live = live_ref[my_clip]
    voxels = jnp.full((8, LANES), live * ((channels // GROUPS) * PLANE * tiles), jnp.int32)
    scaled = sums_in / voxels.astype(F32)
    stat_lane = iota((LANES, channels), 0)
    stat_group = iota((LANES, channels), 1) >> per_group
    mean = dot(scaled, (stat_lane - STAT == stat_group).astype(F32), precision=HIGHEST)
    second = dot(scaled, (stat_lane - STAT - GROUPS == stat_group).astype(F32), precision=HIGHEST)
    scale = lax.rsqrt(second - mean * mean + EPSILON)
    scale = (scale * gain_ref[...])[0:1]
    mean = mean[0:1]
    bias = bias_ref[...]

    def activate(raw):
        v = (raw.astype(F32) - mean) * scale + bias
        u = 0.5 * v
        return u + u * jnp.tanh(u)

    for t in range(LT):
        @pl.loop(0, TH, unroll=2)
        def _(h):
            y = activate(total[pl.ds(pl.multiple_of((t * TH + h) * TW, TW), TW)])
            padded[t, h + 1, :, 0:channels] = pltpu.roll(y, 1, 0).astype(BF16)
            padded[t, h + 1, :, channels : 2 * channels] = y.astype(BF16)
            padded[t, h + 1, :, 2 * channels : 3 * channels] = pltpu.roll(y, TW - 1, 0).astype(BF16)

    for e, (down, right) in enumerate(EDGES):
        @pl.when(exists(-down, -right))
        def _():
            halo_copy(e).wait_recv()

    zero = jnp.zeros((1, channels), F32)
    for e, (down, right) in enumerate(EDGES):
        if 2 <= e < 4:
            continue
        begin, end = (e * 32, e * 32 + 32) if e < 2 else (e * 16, e * 16 + 16)
        edge_act[begin:end] = jnp.where(exists(-down, -right), activate(edge_in[begin:end]), zero)

    where = iota((TW, channels), 0)
    place16 = iota((16, channels), 0)

    @pl.loop(0, LT * TH)
    def _(r):
        t, h = r // TH, r % TH + 1
        head = padded[t, h, 0:16, 0:channels].astype(F32)
        head = jnp.where(place16 == 0, edge_act[pl.ds(r, 1)], head)
        padded[t, h, 0:16, 0:channels] = head.astype(BF16)
        last = padded[t, h, TW - 16 : TW, 2 * channels : 3 * channels].astype(F32)
        last = jnp.where(place16 == 15, edge_act[pl.ds(r + 32, 1)], last)
        padded[t, h, TW - 16 : TW, 2 * channels : 3 * channels] = last.astype(BF16)

    for side in range(2):
        ok = exists(2 * side - 1, 0)
        for t in range(LT):
            y = jnp.where(ok, activate(face_in[side, t * TW : (t + 1) * TW]), zero)
            base = 64 + side * 32 + t
            before_y = jnp.where(where == 0, edge_act[base : base + 1], pltpu.roll(y, 1, 0))
            after_y = jnp.where(
                where == TW - 1, edge_act[base + 16 : base + 17], pltpu.roll(y, TW - 1, 0)
            )
            h = side * (TH + 1)
            padded[t, h, :, 0:channels] = before_y.astype(BF16)
            padded[t, h, :, channels : 2 * channels] = y.astype(BF16)
            padded[t, h, :, 2 * channels : 3 * channels] = after_y.astype(BF16)

    summed[...] = jnp.broadcast_to(out_bias_ref[...], summed.shape)
    for a in range(3):
        @pl.loop(0, 3)
        def _(b):
            frames = LT - 2 + a
            slab = padded[0:frames, pl.ds(b, TH)].reshape(frames * PLANE, 3 * channels)
            summed[(2 - a) * PLANE :, :] += dot(slab, weight_ref[a * 3 + b])

    frame = iota(summed.shape, 0) >> bits(PLANE)
    out_ref[...] = jnp.where(frame < live, summed[...], 0.0).astype(BF16)

    @pl.loop(0, count)
    def _(k):
        @pl.when(k != own)
        def _():
            meta_copy(k).wait_send()
            row_copy(k).wait_send()

    for e, (down, right) in enumerate(EDGES):
        @pl.when(exists(down, right))
        def _():
            halo_copy(e).wait_send()


def on_device(
    seq_rows, plan_owner, plan_slot, live_frames, norm_gain, norm_bias, conv_weight, conv_bias
):
    rows, channels = seq_rows.shape
    out_width = conv_bias.shape[0]
    tiles = lax.axis_size("tile")
    clips = lax.axis_size("clip")
    count = tiles * clips
    cap = -(-(3 * (rows // count) // 2) // 16) * 16
    dma = pltpu.SemaphoreType.DMA
    decoded = pl.pallas_call(
        functools.partial(decode_kernel, tiles, clips, cap),
        out_shape=jax.ShapeDtypeStruct((rows, out_width), BF16),
        in_specs=[pl.BlockSpec(memory_space=pl.ANY)] * 8,
        out_specs=pl.BlockSpec(memory_space=pltpu.VMEM),
        scratch_shapes=[
            pltpu.SMEM((clips,), jnp.int32),
            pltpu.VMEM((1, rows), jnp.int32),
            pltpu.VMEM((1, rows), jnp.int32),
            pltpu.VMEM((rows, channels), BF16),
            pltpu.VMEM((1, channels), F32),
            pltpu.VMEM((1, channels), F32),
            pltpu.VMEM((1, out_width), F32),
            pltpu.VMEM((9, 3 * channels, out_width), BF16),
            pltpu.VMEM((count, cap, channels), BF16),
            pltpu.VMEM((count, cap, channels), BF16),
            pltpu.VMEM((count, 1, LANES), F32),
            pltpu.VMEM((count, 1, LANES), F32),
            pltpu.VMEM((rows, channels), F32),
            pltpu.VMEM((128, channels), BF16),
            pltpu.VMEM((2, LT * TW, channels), BF16),
            pltpu.VMEM((128, channels), BF16),
            pltpu.VMEM((2, LT * TW, channels), BF16),
            pltpu.VMEM((LT, TH + 2, TW, 3 * channels), BF16),
            pltpu.VMEM((rows, out_width), F32),
            pltpu.VMEM((128, channels), F32),
            dma((8,)),
            dma((count,)),
            dma((count,)),
            dma((count,)),
            dma((count,)),
            dma((8,)),
            dma((8,)),
        ],
        compiler_params=pltpu.CompilerParams(
            collective_id=0, has_side_effects=True, vmem_limit_bytes=56 << 20
        ),
        name="decode",
    )(
        live_frames,
        plan_owner.reshape(1, rows),
        plan_slot.reshape(1, rows),
        seq_rows,
        norm_gain.reshape(1, channels),
        norm_bias.reshape(1, channels),
        conv_bias.reshape(1, out_width),
        conv_weight.transpose(0, 1, 3, 2, 4).reshape(9, 3 * channels, out_width),
    )
    return decoded.reshape(1, 1, LT, TH, TW, out_width)


def solution(mesh):
    return jax.shard_map(
        on_device,
        mesh=mesh,
        in_specs=(
            P(("tile", "clip"), None),
            P(("tile", "clip")),
            P(("tile", "clip")),
            P(),
            P(),
            P(),
            P(),
            P(),
        ),
        out_specs=P("clip", "tile", None, None, None, None),
        check_vma=False,
    )
```

```python
import functools

import jax
import jax.numpy as jnp
from jax import lax
from jax.experimental import pallas as pl
from jax.experimental.pallas import tpu as pltpu
from jax.sharding import PartitionSpec as P

GROUPS = 32
LT = 4
TH = 8
TW = 32
GW = 4
PLANE = TH * TW
LANES = 128
STAT = 64
EPSILON = 1e-06
HIGHEST = lax.Precision.HIGHEST
F32 = jnp.float32
BF16 = jnp.bfloat16
NT = (((1,), (1,)), ((), ()))
MESH = pl.DeviceIdType.MESH
EDGES = ((0, 1), (0, -1), (1, 0), (-1, 0), (1, 1), (1, -1), (-1, 1), (-1, -1))


def iota(shape, axis):
    return lax.broadcasted_iota(jnp.int32, shape, axis)


def bits(n):
    return n.bit_length() - 1


def dot(a, b, **kw):
    return jnp.dot(a, b, preferred_element_type=F32, **kw)


def decode_kernel(
    tiles,
    clips,
    cap,
    live_hbm,
    owner_hbm,
    slot_hbm,
    rows_hbm,
    gain_hbm,
    bias_hbm,
    out_bias_hbm,
    weight_hbm,
    out_ref,
    live_ref,
    owner_ref,
    slot_ref,
    rows_ref,
    gain_ref,
    bias_ref,
    out_bias_ref,
    weight_ref,
    send_rows,
    recv_rows,
    send_meta,
    recv_meta,
    total,
    edge_out,
    face_out,
    edge_in,
    face_in,
    padded,
    summed,
    edge_act,
    loaded,
    row_sent,
    row_got,
    meta_sent,
    meta_got,
    halo_sent,
    halo_got,
):
    loads = [
        pltpu.make_async_copy(source, target, loaded.at[i])
        for i, (source, target) in enumerate(
            (
                (owner_hbm, owner_ref),
                (slot_hbm, slot_ref),
                (live_hbm, live_ref),
                (rows_hbm, rows_ref),
                (gain_hbm, gain_ref),
                (bias_hbm, bias_ref),
                (out_bias_hbm, out_bias_ref),
                (weight_hbm, weight_ref),
            )
        )
    ]
    for load in loads[:-1]:
        load.start()
    count = tiles * clips
    half = tiles // 2
    own = 1
    rows, channels = rows_ref.shape
    my_tile = lax.axis_index("tile")
    my_clip = lax.axis_index("clip")
    my_half = my_tile // half
    my_local = my_tile % half

    def partner(k):
        rest = k // 2
        to_half = (my_half + 1 + k % 2) % 2
        to_tile = to_half * half + (my_local + rest // clips) % half
        return to_tile, (my_clip + rest % clips) % clips

    for buffer in (edge_in, face_in):
        buffer[...] = jnp.zeros_like(buffer)
    barrier = pltpu.get_barrier_semaphore()

    @pl.loop(0, count)
    def _(k):
        @pl.when(k != own)
        def _():
            pl.semaphore_signal(barrier, inc=1, device_id=partner(k), device_id_type=MESH)

    for load in loads[:4]:
        load.wait()
    owner = owner_ref[...]
    slot = slot_ref[...]
    table = (iota((count, rows), 0) == owner).astype(F32)
    before = (iota((rows, rows), 0) < iota((rows, rows), 1)).astype(F32).astype(BF16)
    rank = jnp.sum(dot(table.astype(BF16), before) * table, axis=0, keepdims=True)
    to_clip = owner >> bits(tiles)
    to_tile = owner & (tiles - 1)
    same = ((to_tile >> bits(half)) == my_half).astype(jnp.int32)
    turn = ((to_tile & (half - 1)) - my_local) & (half - 1)
    order = 2 * (turn * clips + ((to_clip - my_clip) & (clips - 1))) + same
    position = order * cap + rank.astype(jnp.int32)

    values = rows_ref[...]
    per_group = bits(channels // GROUPS)

    digits_row = iota((8, rows), 0)
    digits = jnp.where(digits_row == 0, slot >> 5, jnp.where(digits_row == 1, slot & 31, 0))
    digits = digits.astype(F32).astype(BF16)

    batch = max(2 * clips, min(count, 512 // cap // 8 * 8))
    size = batch * cap
    segment = iota((batch, size), 0) * cap
    column = iota((batch, size), 1)
    inside = (column >= segment) & (column < segment + cap)
    piece = (iota((cap, LANES), 0) == iota((cap, LANES), 1)).astype(F32).astype(BF16)
    place = jnp.concatenate([piece] * batch, axis=0)

    def row_copy(k):
        return pltpu.make_async_remote_copy(
            src_ref=send_rows.at[k],
            dst_ref=recv_rows.at[k],
            send_sem=row_sent.at[k],
            recv_sem=row_got.at[k],
            device_id=partner(k),
            device_id_type=MESH,
        )

    def meta_copy(k):
        return pltpu.make_async_remote_copy(
            src_ref=send_meta.at[k],
            dst_ref=recv_meta.at[k],
            send_sem=meta_sent.at[k],
            recv_sem=meta_got.at[k],
            device_id=partner(k),
            device_id_type=MESH,
        )

    def partial_sums():
        clip_row = iota((8, rows), 0)
        live_limit = jnp.zeros((8, rows), jnp.int32)
        for c in range(clips):
            live_limit = jnp.where(clip_row == c, live_ref[c] * PLANE, live_limit)
        mask = ((clip_row == to_clip) & (slot < live_limit)).astype(F32).astype(BF16)
        wide = values.astype(F32)
        square = wide * wide
        high = square.astype(BF16)
        low = (square - high.astype(F32)).astype(BF16)
        sum1 = dot(mask, values)
        sum2 = dot(mask, high) + dot(mask, low)
        group = iota((channels, LANES), 0) >> per_group
        lane = iota((channels, LANES), 1)
        partial = dot(sum1, (lane - STAT == group).astype(F32), precision=HIGHEST) + dot(
            sum2, (lane - STAT - GROUPS == group).astype(F32), precision=HIGHEST
        )

        goes = (my_clip + (iota((batch, LANES), 0) >> 1)) & (clips - 1)
        stats = jnp.zeros((batch, LANES), F32)
        for c in range(clips):
            stats = jnp.where(goes == c, partial[c : c + 1], stats)
        return stats

    for step in range(count // batch):
        first = step * batch
        chosen = (iota((size, rows), 0) + first * cap == position).astype(F32).astype(BF16)
        packed = dot(chosen, values).astype(BF16)
        send_rows[first : first + batch] = packed.reshape(batch, cap, channels)
        if first <= own < first + batch:
            recv_rows[own] = send_rows[own]
        if step == 0:
            pl.semaphore_wait(barrier, count - 1)

        @pl.loop(first, first + batch)
        def _(k):
            @pl.when(k != own)
            def _():
                row_copy(k).start()

        if step == 0:
            stats = partial_sums()
        slots = lax.dot_general(digits, chosen, NT, preferred_element_type=F32)
        upper = jnp.where(inside, slots[0:1], 0.0).astype(BF16)
        lower = jnp.where(inside, slots[1:2], 0.0).astype(BF16)
        meta = dot(upper, place) * 32.0 + dot(lower, place) + stats
        for i in range(batch):
            send_meta[first + i] = meta[i : i + 1]
        if first <= own < first + batch:
            recv_meta[own] = send_meta[own]

        @pl.loop(first, first + batch)
        def _(k):
            @pl.when(k != own)
            def _():
                meta_copy(k).start()

    loads[-1].start()

    joint = max(1, min(count, 256 // cap))
    while count % joint:
        joint -= 1
    width = joint * cap
    spread_lane = iota((LANES, width), 0)
    spread_col = iota((LANES, width), 1)
    spread = jnp.zeros((LANES, width), F32)
    owner_of = jnp.zeros((8, width), jnp.int32)
    for m in range(joint):
        hit = (spread_col - m * cap == spread_lane) & (spread_lane < cap)
        spread = jnp.where(hit, 1.0, spread)
        owner_of = jnp.where(iota((8, width), 1) >= m * cap, m, owner_of)
    voxel = iota((rows, width), 0)
    sums_in = jnp.zeros((1, LANES), F32)
    depth = (joint + 7) // 8
    for step in range(count // joint):
        first = step * joint

        @pl.loop(first, first + joint)
        def _(k):
            @pl.when(k != own)
            def _():
                meta_copy(k).wait_recv()
                row_copy(k).wait_recv()

        slot_row = jnp.zeros((1, width), F32)
        for d in range(depth):
            metas = jnp.zeros((8, LANES), F32)
            for m in range(d * 8, min(joint, d * 8 + 8)):
                one = recv_meta[first + m]
                sums_in = sums_in + one
                metas = jnp.where(iota((8, LANES), 0) == m - d * 8, one, metas)
            moved = dot(metas, spread, precision=HIGHEST)
            keep = owner_of == iota((8, width), 0) + d * 8
            slot_row = slot_row + jnp.sum(jnp.where(keep, moved, 0.0), axis=0, keepdims=True)
        target = (voxel == (slot_row + 0.5).astype(jnp.int32)).astype(F32).astype(BF16)
        arrived = recv_rows[first : first + joint].reshape(width, channels)
        placed = dot(target, arrived)
        if step == 0:
            total[...] = placed
        else:
            total[...] += placed

    tile = total[...].astype(BF16)
    grid = tile.reshape(LT, TH, TW, channels)
    face_out[0] = grid[:, TH - 1].reshape(LT * TW, channels)
    face_out[1] = grid[:, 0].reshape(LT * TW, channels)
    line = iota((128, rows), 0)
    source = iota((128, rows), 1)
    wanted = jnp.where(
        line < 32,
        line * TW + TW - 1,
        jnp.where(line < 64, (line - 32) * TW, -1),
    )
    for e, (down, right) in enumerate(EDGES[4:]):
        base = 64 + e * 16
        offset = (TH - 1 if down > 0 else 0) * TW + (TW - 1 if right > 0 else 0)
        in_corner = (line >= base) & (line < base + LT)
        wanted = jnp.where(in_corner, (line - base) * PLANE + offset, wanted)
    edges = dot((source == wanted).astype(F32).astype(BF16), tile).astype(BF16)
    edge_out[...] = edges

    grid_rows = tiles // GW
    row_tile = my_tile // GW
    column_tile = my_tile % GW

    def exists(down, right):
        row = row_tile + down
        column = column_tile + right
        return (row >= 0) & (row < grid_rows) & (column >= 0) & (column < GW)

    def halo_copy(e):
        down, right = EDGES[e]
        if e < 2:
            part, source_ref, target_ref = pl.ds(e * 32, 32), edge_out, edge_in
        elif e < 4:
            part, source_ref, target_ref = e - 2, face_out, face_in
        else:
            part, source_ref, target_ref = pl.ds(64 + (e - 4) * 16, 16), edge_out, edge_in
        return pltpu.make_async_remote_copy(
            src_ref=source_ref.at[part],
            dst_ref=target_ref.at[part],
            send_sem=halo_sent.at[e],
            recv_sem=halo_got.at[e],
            device_id=(my_tile + down * GW + right, my_clip),
            device_id_type=MESH,
        )

    for e in (0, 1, 2, 3, 4, 5, 6, 7):
        @pl.when(exists(*EDGES[e]))
        def _():
            halo_copy(e).start()

    for load in loads[4:]:
        load.wait()
    live = live_ref[my_clip]
    voxels = jnp.full((8, LANES), live * ((channels // GROUPS) * PLANE * tiles), jnp.int32)
    scaled = sums_in / voxels.astype(F32)
    stat_lane = iota((LANES, channels), 0)
    stat_group = iota((LANES, channels), 1) >> per_group
    mean = dot(scaled, (stat_lane - STAT == stat_group).astype(F32), precision=HIGHEST)
    second = dot(scaled, (stat_lane - STAT - GROUPS == stat_group).astype(F32), precision=HIGHEST)
    scale = lax.rsqrt(second - mean * mean + EPSILON)
    scale = (scale * gain_ref[...])[0:1]
    mean = mean[0:1]
    bias = bias_ref[...]

    def activate(raw):
        v = (raw.astype(F32) - mean) * scale + bias
        u = 0.5 * v
        return u + u * jnp.tanh(u)

    for t in range(LT):
        @pl.loop(0, TH, unroll=2)
        def _(h):
            y = activate(total[pl.ds(pl.multiple_of((t * TH + h) * TW, TW), TW)])
            padded[t, h + 1, :, 0:channels] = pltpu.roll(y, 1, 0).astype(BF16)
            padded[t, h + 1, :, channels : 2 * channels] = y.astype(BF16)
            padded[t, h + 1, :, 2 * channels : 3 * channels] = pltpu.roll(y, TW - 1, 0).astype(BF16)

    zero = jnp.zeros((1, channels), F32)

    def receive(e):
        down, right = EDGES[e]

        @pl.when(exists(-down, -right))
        def _():
            halo_copy(e).wait_recv()

        if 2 <= e < 4:
            return
        begin, end = (e * 32, e * 32 + 32) if e < 2 else (e * 16, e * 16 + 16)
        edge_act[begin:end] = jnp.where(exists(-down, -right), activate(edge_in[begin:end]), zero)

    receive(0)
    receive(1)
    place16 = iota((16, channels), 0)

    @pl.loop(0, LT * TH)
    def _(r):
        t, h = r // TH, r % TH + 1
        head = padded[t, h, 0:16, 0:channels].astype(F32)
        head = jnp.where(place16 == 0, edge_act[pl.ds(r, 1)], head)
        padded[t, h, 0:16, 0:channels] = head.astype(BF16)
        last = padded[t, h, TW - 16 : TW, 2 * channels : 3 * channels].astype(F32)
        last = jnp.where(place16 == 15, edge_act[pl.ds(r + 32, 1)], last)
        padded[t, h, TW - 16 : TW, 2 * channels : 3 * channels] = last.astype(BF16)

    summed[...] = jnp.broadcast_to(out_bias_ref[...], summed.shape)
    width_in = 3 * channels
    for a in range(3):
        @pl.loop(0, 3)
        def _(b):
            frames = LT - 2 + a
            slab = padded[0:frames, pl.ds(b + 1, TH - 2)]
            product = dot(slab.reshape(frames * (TH - 2) * TW, width_in), weight_ref[a * 3 + b])
            summed[2 - a :, 1 : TH - 1] += product.reshape(frames, TH - 2, TW, -1)

    for e in range(2, 8):
        receive(e)
    where = iota((TW, channels), 0)
    for side in range(2):
        ok = exists(2 * side - 1, 0)
        for t in range(LT):
            y = jnp.where(ok, activate(face_in[side, t * TW : (t + 1) * TW]), zero)
            base = 64 + side * 32 + t
            before_y = jnp.where(where == 0, edge_act[base : base + 1], pltpu.roll(y, 1, 0))
            after_y = jnp.where(
                where == TW - 1, edge_act[base + 16 : base + 17], pltpu.roll(y, TW - 1, 0)
            )
            h = side * (TH + 1)
            padded[t, h, :, 0:channels] = before_y.astype(BF16)
            padded[t, h, :, channels : 2 * channels] = y.astype(BF16)
            padded[t, h, :, 2 * channels : 3 * channels] = after_y.astype(BF16)

    for a in range(3):
        @pl.loop(0, 3)
        def _(b):
            frames = LT - 2 + a
            slab = jnp.concatenate([padded[0:frames, b], padded[0:frames, b + TH - 1]], axis=0)
            product = dot(slab.reshape(2 * frames * TW, width_in), weight_ref[a * 3 + b])
            product = product.reshape(2 * frames, TW, -1)
            summed[2 - a :, 0] += product[:frames]
            summed[2 - a :, TH - 1] += product[frames:]

    frame = iota(summed.shape, 0)
    decoded = jnp.where(frame < live, summed[...], 0.0).astype(BF16)
    out_ref[...] = decoded.reshape(out_ref.shape)

    @pl.loop(0, count)
    def _(k):
        @pl.when(k != own)
        def _():
            meta_copy(k).wait_send()
            row_copy(k).wait_send()

    for e, (down, right) in enumerate(EDGES):
        @pl.when(exists(down, right))
        def _():
            halo_copy(e).wait_send()


def on_device(
    seq_rows, plan_owner, plan_slot, live_frames, norm_gain, norm_bias, conv_weight, conv_bias
):
    rows, channels = seq_rows.shape
    out_width = conv_bias.shape[0]
    tiles = lax.axis_size("tile")
    clips = lax.axis_size("clip")
    count = tiles * clips
    cap = -(-(3 * (rows // count) // 2) // 16) * 16
    dma = pltpu.SemaphoreType.DMA
    decoded = pl.pallas_call(
        functools.partial(decode_kernel, tiles, clips, cap),
        out_shape=jax.ShapeDtypeStruct((rows, out_width), BF16),
        in_specs=[pl.BlockSpec(memory_space=pltpu.HBM)] * 8,
        out_specs=pl.BlockSpec(memory_space=pltpu.VMEM),
        scratch_shapes=[
            pltpu.SMEM((clips,), jnp.int32),
            pltpu.VMEM((1, rows), jnp.int32),
            pltpu.VMEM((1, rows), jnp.int32),
            pltpu.VMEM((rows, channels), BF16),
            pltpu.VMEM((1, channels), F32),
            pltpu.VMEM((1, channels), F32),
            pltpu.VMEM((1, out_width), F32),
            pltpu.VMEM((9, 3 * channels, out_width), BF16),
            pltpu.VMEM((count, cap, channels), BF16),
            pltpu.VMEM((count, cap, channels), BF16),
            pltpu.VMEM((count, 1, LANES), F32),
            pltpu.VMEM((count, 1, LANES), F32),
            pltpu.VMEM((rows, channels), F32),
            pltpu.VMEM((128, channels), BF16),
            pltpu.VMEM((2, LT * TW, channels), BF16),
            pltpu.VMEM((128, channels), BF16),
            pltpu.VMEM((2, LT * TW, channels), BF16),
            pltpu.VMEM((LT, TH + 2, TW, 3 * channels), BF16),
            pltpu.VMEM((LT, TH, TW, out_width), F32),
            pltpu.VMEM((128, channels), F32),
            dma((8,)),
            dma((count,)),
            dma((count,)),
            dma((count,)),
            dma((count,)),
            dma((8,)),
            dma((8,)),
        ],
        compiler_params=pltpu.CompilerParams(
            collective_id=0, has_side_effects=True, vmem_limit_bytes=56 << 20
        ),
        name="decode",
    )(
        live_frames,
        plan_owner.reshape(1, rows),
        plan_slot.reshape(1, rows),
        seq_rows,
        norm_gain.reshape(1, channels),
        norm_bias.reshape(1, channels),
        conv_bias.reshape(1, out_width),
        conv_weight.transpose(0, 1, 3, 2, 4).reshape(9, 3 * channels, out_width),
    )
    return decoded.reshape(1, 1, LT, TH, TW, out_width)


def solution(mesh):
    return jax.shard_map(
        on_device,
        mesh=mesh,
        in_specs=(
            P(("tile", "clip"), None),
            P(("tile", "clip")),
            P(("tile", "clip")),
            P(),
            P(),
            P(),
            P(),
            P(),
        ),
        out_specs=P("clip", "tile", None, None, None, None),
        check_vma=False,
    )
```

```python
import functools

import jax
import jax.numpy as jnp
from jax import lax
from jax.experimental import pallas as pl
from jax.experimental.pallas import tpu as pltpu
from jax.sharding import PartitionSpec as P

GROUPS = 32
LT = 4
TH = 8
TW = 32
GW = 4
PLANE = TH * TW
LANES = 128
STAT = 64
EPSILON = 1e-06
HIGHEST = lax.Precision.HIGHEST
F32 = jnp.float32
BF16 = jnp.bfloat16
NT = (((1,), (1,)), ((), ()))
MESH = pl.DeviceIdType.MESH
EDGES = ((0, 1), (0, -1), (1, 0), (-1, 0), (1, 1), (1, -1), (-1, 1), (-1, -1))


def iota(shape, axis):
    return lax.broadcasted_iota(jnp.int32, shape, axis)


def bits(n):
    return n.bit_length() - 1


def dot(a, b, **kw):
    return jnp.dot(a, b, preferred_element_type=F32, **kw)


def decode_kernel(
    tiles,
    clips,
    cap,
    live_hbm,
    owner_hbm,
    slot_hbm,
    rows_hbm,
    gain_hbm,
    bias_hbm,
    out_bias_hbm,
    weight_hbm,
    out_ref,
    live_ref,
    owner_ref,
    slot_ref,
    rows_ref,
    gain_ref,
    bias_ref,
    out_bias_ref,
    weight_ref,
    send_rows,
    recv_rows,
    send_meta,
    recv_meta,
    total,
    edge_out,
    face_out,
    edge_in,
    face_in,
    padded,
    summed,
    edge_act,
    loaded,
    row_sent,
    row_got,
    meta_sent,
    meta_got,
    halo_sent,
    halo_got,
):
    loads = [
        pltpu.make_async_copy(source, target, loaded.at[i])
        for i, (source, target) in enumerate(
            (
                (owner_hbm, owner_ref),
                (slot_hbm, slot_ref),
                (live_hbm, live_ref),
                (rows_hbm, rows_ref),
                (gain_hbm, gain_ref),
                (bias_hbm, bias_ref),
                (out_bias_hbm, out_bias_ref),
                (weight_hbm, weight_ref),
            )
        )
    ]
    for load in loads[:-1]:
        load.start()
    count = tiles * clips
    half = tiles // 2
    own = 1
    rows, channels = rows_ref.shape
    my_tile = lax.axis_index("tile")
    my_clip = lax.axis_index("clip")
    my_half = my_tile // half
    my_local = my_tile % half

    def partner(k):
        rest = lax.div(k, 2)
        to_half = lax.rem(my_half + 1 + lax.rem(k, 2), 2)
        to_tile = to_half * half + lax.rem(my_local + lax.div(rest, clips), half)
        return to_tile, lax.rem(my_clip + lax.rem(rest, clips), clips)

    for buffer in (edge_in, face_in):
        buffer[...] = jnp.zeros_like(buffer)
    barrier = pltpu.get_barrier_semaphore()

    @pl.loop(0, count)
    def _(k):
        @pl.when(k != own)
        def _():
            pl.semaphore_signal(barrier, inc=1, device_id=partner(k), device_id_type=MESH)

    before = (iota((rows, rows), 0) < iota((rows, rows), 1)).astype(F32).astype(BF16)
    for load in loads[:2]:
        load.wait()
    owner = owner_ref[...]
    slot = slot_ref[...]
    table = (iota((count, rows), 0) == owner).astype(F32)
    rank = jnp.sum(dot(table.astype(BF16), before) * table, axis=0, keepdims=True)
    to_clip = owner >> bits(tiles)
    to_tile = owner & (tiles - 1)
    same = ((to_tile >> bits(half)) == my_half).astype(jnp.int32)
    turn = ((to_tile & (half - 1)) - my_local) & (half - 1)
    order = 2 * (turn * clips + ((to_clip - my_clip) & (clips - 1))) + same
    position = order * cap + rank.astype(jnp.int32)

    for load in loads[2:4]:
        load.wait()
    values = rows_ref[...]
    per_group = bits(channels // GROUPS)

    digits_row = iota((8, rows), 0)
    digits = jnp.where(digits_row == 0, slot >> 5, jnp.where(digits_row == 1, slot & 31, 0))
    digits = digits.astype(F32).astype(BF16)

    batch = max(2 * clips, min(count, 512 // cap // 8 * 8))
    size = batch * cap
    segment = iota((batch, size), 0) * cap
    column = iota((batch, size), 1)
    inside = (column >= segment) & (column < segment + cap)
    piece = (iota((cap, LANES), 0) == iota((cap, LANES), 1)).astype(F32).astype(BF16)
    place = jnp.concatenate([piece] * batch, axis=0)

    def row_copy(k):
        return pltpu.make_async_remote_copy(
            src_ref=send_rows.at[k],
            dst_ref=recv_rows.at[k],
            send_sem=row_sent.at[k],
            recv_sem=row_got.at[k],
            device_id=partner(k),
            device_id_type=MESH,
        )

    def meta_copy(k):
        return pltpu.make_async_remote_copy(
            src_ref=send_meta.at[k],
            dst_ref=recv_meta.at[k],
            send_sem=meta_sent.at[k],
            recv_sem=meta_got.at[k],
            device_id=partner(k),
            device_id_type=MESH,
        )

    def partial_sums():
        clip_row = iota((8, rows), 0)
        live_limit = jnp.zeros((8, rows), jnp.int32)
        for c in range(clips):
            live_limit = jnp.where(clip_row == c, live_ref[c] * PLANE, live_limit)
        mask = ((clip_row == to_clip) & (slot < live_limit)).astype(F32).astype(BF16)
        wide = values.astype(F32)
        square = wide * wide
        high = square.astype(BF16)
        low = (square - high.astype(F32)).astype(BF16)
        sum1 = dot(mask, values)
        sum2 = dot(mask, high) + dot(mask, low)
        group = iota((channels, LANES), 0) >> per_group
        lane = iota((channels, LANES), 1)
        partial = dot(sum1, (lane - STAT == group).astype(F32), precision=HIGHEST) + dot(
            sum2, (lane - STAT - GROUPS == group).astype(F32), precision=HIGHEST
        )

        goes = (my_clip + (iota((batch, LANES), 0) >> 1)) & (clips - 1)
        stats = jnp.zeros((batch, LANES), F32)
        for c in range(clips):
            stats = jnp.where(goes == c, partial[c : c + 1], stats)
        return stats

    for step in range(count // batch):
        first = step * batch
        chosen = (iota((size, rows), 0) + first * cap == position).astype(F32).astype(BF16)
        packed = dot(chosen, values).astype(BF16)
        send_rows[first : first + batch] = packed.reshape(batch, cap, channels)
        if first <= own < first + batch:
            recv_rows[own] = send_rows[own]
        if step == 0:
            pl.semaphore_wait(barrier, count - 1)

        @pl.loop(first, first + batch)
        def _(k):
            @pl.when(k != own)
            def _():
                row_copy(k).start()

        if step == 0:
            stats = partial_sums()
        slots = lax.dot_general(digits, chosen, NT, preferred_element_type=F32)
        upper = jnp.where(inside, slots[0:1], 0.0).astype(BF16)
        lower = jnp.where(inside, slots[1:2], 0.0).astype(BF16)
        meta = dot(upper, place) * 32.0 + dot(lower, place) + stats
        for i in range(batch):
            send_meta[first + i] = meta[i : i + 1]
        if first <= own < first + batch:
            recv_meta[own] = send_meta[own]

        @pl.loop(first, first + batch)
        def _(k):
            @pl.when(k != own)
            def _():
                meta_copy(k).start()

    loads[-1].start()

    joint = max(1, min(count, 256 // cap))
    while count % joint:
        joint -= 1
    width = joint * cap
    spread_lane = iota((LANES, width), 0)
    spread_col = iota((LANES, width), 1)
    spread = jnp.zeros((LANES, width), F32)
    owner_of = jnp.zeros((8, width), jnp.int32)
    for m in range(joint):
        hit = (spread_col - m * cap == spread_lane) & (spread_lane < cap)
        spread = jnp.where(hit, 1.0, spread)
        owner_of = jnp.where(iota((8, width), 1) >= m * cap, m, owner_of)
    voxel = iota((rows, width), 0)
    sums_in = jnp.zeros((1, LANES), F32)
    depth = (joint + 7) // 8
    for step in range(count // joint):
        first = step * joint

        @pl.loop(first, first + joint)
        def _(k):
            @pl.when(k != own)
            def _():
                meta_copy(k).wait_recv()
                row_copy(k).wait_recv()

        slot_row = jnp.zeros((1, width), F32)
        for d in range(depth):
            metas = jnp.zeros((8, LANES), F32)
            for m in range(d * 8, min(joint, d * 8 + 8)):
                one = recv_meta[first + m]
                sums_in = sums_in + one
                metas = jnp.where(iota((8, LANES), 0) == m - d * 8, one, metas)
            moved = dot(metas, spread, precision=HIGHEST)
            keep = owner_of == iota((8, width), 0) + d * 8
            slot_row = slot_row + jnp.sum(jnp.where(keep, moved, 0.0), axis=0, keepdims=True)
        target = (voxel == (slot_row + 0.5).astype(jnp.int32)).astype(F32).astype(BF16)
        arrived = recv_rows[first : first + joint].reshape(width, channels)
        placed = dot(target, arrived)
        if step == 0:
            total[...] = placed
        else:
            total[...] += placed

    tile = total[...].astype(BF16)
    grid = tile.reshape(LT, TH, TW, channels)
    face_out[0] = grid[:, TH - 1].reshape(LT * TW, channels)
    face_out[1] = grid[:, 0].reshape(LT * TW, channels)
    line = iota((128, rows), 0)
    source = iota((128, rows), 1)
    wanted = jnp.where(
        line < 32,
        line * TW + TW - 1,
        jnp.where(line < 64, (line - 32) * TW, -1),
    )
    for e, (down, right) in enumerate(EDGES[4:]):
        base = 64 + e * 16
        offset = (TH - 1 if down > 0 else 0) * TW + (TW - 1 if right > 0 else 0)
        in_corner = (line >= base) & (line < base + LT)
        wanted = jnp.where(in_corner, (line - base) * PLANE + offset, wanted)
    edges = dot((source == wanted).astype(F32).astype(BF16), tile).astype(BF16)
    edge_out[...] = edges

    grid_rows = tiles // GW
    row_tile = my_tile // GW
    column_tile = my_tile % GW

    def exists(down, right):
        row = row_tile + down
        column = column_tile + right
        return (row >= 0) & (row < grid_rows) & (column >= 0) & (column < GW)

    def halo_copy(e):
        down, right = EDGES[e]
        if e < 2:
            part, source_ref, target_ref = pl.ds(e * 32, 32), edge_out, edge_in
        elif e < 4:
            part, source_ref, target_ref = e - 2, face_out, face_in
        else:
            part, source_ref, target_ref = pl.ds(64 + (e - 4) * 16, 16), edge_out, edge_in
        return pltpu.make_async_remote_copy(
            src_ref=source_ref.at[part],
            dst_ref=target_ref.at[part],
            send_sem=halo_sent.at[e],
            recv_sem=halo_got.at[e],
            device_id=(my_tile + down * GW + right, my_clip),
            device_id_type=MESH,
        )

    for e in (0, 1, 2, 3, 4, 5, 6, 7):
        @pl.when(exists(*EDGES[e]))
        def _():
            halo_copy(e).start()

    for load in loads[4:]:
        load.wait()
    live = live_ref[my_clip]
    voxels = jnp.full((8, LANES), live * ((channels // GROUPS) * PLANE * tiles), jnp.int32)
    scaled = sums_in / voxels.astype(F32)
    stat_lane = iota((LANES, channels), 0)
    stat_group = iota((LANES, channels), 1) >> per_group
    mean = dot(scaled, (stat_lane - STAT == stat_group).astype(F32), precision=HIGHEST)
    second = dot(scaled, (stat_lane - STAT - GROUPS == stat_group).astype(F32), precision=HIGHEST)
    scale = lax.rsqrt(second - mean * mean + EPSILON)
    scale = (scale * gain_ref[...])[0:1]
    mean = mean[0:1]
    bias = bias_ref[...]

    def activate(raw):
        v = (raw.astype(F32) - mean) * scale + bias
        u = 0.5 * v
        return u + u * jnp.tanh(u)

    for t in range(LT):
        @pl.loop(0, TH, unroll=2)
        def _(h):
            y = activate(total[pl.ds(pl.multiple_of((t * TH + h) * TW, TW), TW)])
            padded[t, h + 1, :, 0:channels] = pltpu.roll(y, 1, 0).astype(BF16)
            padded[t, h + 1, :, channels : 2 * channels] = y.astype(BF16)
            padded[t, h + 1, :, 2 * channels : 3 * channels] = pltpu.roll(y, TW - 1, 0).astype(BF16)

    zero = jnp.zeros((1, channels), F32)

    def receive(e):
        down, right = EDGES[e]

        @pl.when(exists(-down, -right))
        def _():
            halo_copy(e).wait_recv()

        if 2 <= e < 4:
            return
        begin, end = (e * 32, e * 32 + 32) if e < 2 else (e * 16, e * 16 + 16)
        edge_act[begin:end] = jnp.where(exists(-down, -right), activate(edge_in[begin:end]), zero)

    receive(0)
    receive(1)
    place16 = iota((16, channels), 0)

    @pl.loop(0, LT * TH)
    def _(r):
        t, h = r // TH, r % TH + 1
        head = padded[t, h, 0:16, 0:channels].astype(F32)
        head = jnp.where(place16 == 0, edge_act[pl.ds(r, 1)], head)
        padded[t, h, 0:16, 0:channels] = head.astype(BF16)
        last = padded[t, h, TW - 16 : TW, 2 * channels : 3 * channels].astype(F32)
        last = jnp.where(place16 == 15, edge_act[pl.ds(r + 32, 1)], last)
        padded[t, h, TW - 16 : TW, 2 * channels : 3 * channels] = last.astype(BF16)

    summed[...] = jnp.broadcast_to(out_bias_ref[...], summed.shape)
    width_in = 3 * channels
    for a in range(3):
        @pl.loop(0, 3)
        def _(b):
            frames = LT - 2 + a
            slab = padded[0:frames, pl.ds(b + 1, TH - 2)]
            product = dot(slab.reshape(frames * (TH - 2) * TW, width_in), weight_ref[a * 3 + b])
            summed[2 - a :, 1 : TH - 1] += product.reshape(frames, TH - 2, TW, -1)

    for e in range(2, 8):
        receive(e)
    where = iota((TW, channels), 0)
    for side in range(2):
        ok = exists(2 * side - 1, 0)
        for t in range(LT):
            y = jnp.where(ok, activate(face_in[side, t * TW : (t + 1) * TW]), zero)
            base = 64 + side * 32 + t
            before_y = jnp.where(where == 0, edge_act[base : base + 1], pltpu.roll(y, 1, 0))
            after_y = jnp.where(
                where == TW - 1, edge_act[base + 16 : base + 17], pltpu.roll(y, TW - 1, 0)
            )
            h = side * (TH + 1)
            padded[t, h, :, 0:channels] = before_y.astype(BF16)
            padded[t, h, :, channels : 2 * channels] = y.astype(BF16)
            padded[t, h, :, 2 * channels : 3 * channels] = after_y.astype(BF16)

    for a in range(3):
        @pl.loop(0, 3)
        def _(b):
            frames = LT - 2 + a
            slab = jnp.concatenate([padded[0:frames, b], padded[0:frames, b + TH - 1]], axis=0)
            product = dot(slab.reshape(2 * frames * TW, width_in), weight_ref[a * 3 + b])
            product = product.reshape(2 * frames, TW, -1)
            summed[2 - a :, 0] += product[:frames]
            summed[2 - a :, TH - 1] += product[frames:]

    frame = iota(summed.shape, 0)
    decoded = jnp.where(frame < live, summed[...], 0.0).astype(BF16)
    out_ref[...] = decoded.reshape(out_ref.shape)

    @pl.loop(0, count)
    def _(k):
        @pl.when(k != own)
        def _():
            meta_copy(k).wait_send()
            row_copy(k).wait_send()

    for e, (down, right) in enumerate(EDGES):
        @pl.when(exists(down, right))
        def _():
            halo_copy(e).wait_send()


def on_device(
    seq_rows, plan_owner, plan_slot, live_frames, norm_gain, norm_bias, conv_weight, conv_bias
):
    rows, channels = seq_rows.shape
    out_width = conv_bias.shape[0]
    tiles = lax.axis_size("tile")
    clips = lax.axis_size("clip")
    count = tiles * clips
    cap = -(-(3 * (rows // count) // 2) // 16) * 16
    dma = pltpu.SemaphoreType.DMA
    decoded = pl.pallas_call(
        functools.partial(decode_kernel, tiles, clips, cap),
        out_shape=jax.ShapeDtypeStruct((rows, out_width), BF16),
        in_specs=[pl.BlockSpec(memory_space=pltpu.HBM)] * 8,
        out_specs=pl.BlockSpec(memory_space=pltpu.VMEM),
        scratch_shapes=[
            pltpu.SMEM((clips,), jnp.int32),
            pltpu.VMEM((1, rows), jnp.int32),
            pltpu.VMEM((1, rows), jnp.int32),
            pltpu.VMEM((rows, channels), BF16),
            pltpu.VMEM((1, channels), F32),
            pltpu.VMEM((1, channels), F32),
            pltpu.VMEM((1, out_width), F32),
            pltpu.VMEM((9, 3 * channels, out_width), BF16),
            pltpu.VMEM((count, cap, channels), BF16),
            pltpu.VMEM((count, cap, channels), BF16),
            pltpu.VMEM((count, 1, LANES), F32),
            pltpu.VMEM((count, 1, LANES), F32),
            pltpu.VMEM((rows, channels), F32),
            pltpu.VMEM((128, channels), BF16),
            pltpu.VMEM((2, LT * TW, channels), BF16),
            pltpu.VMEM((128, channels), BF16),
            pltpu.VMEM((2, LT * TW, channels), BF16),
            pltpu.VMEM((LT, TH + 2, TW, 3 * channels), BF16),
            pltpu.VMEM((LT, TH, TW, out_width), F32),
            pltpu.VMEM((128, channels), F32),
            dma((8,)),
            dma((count,)),
            dma((count,)),
            dma((count,)),
            dma((count,)),
            dma((8,)),
            dma((8,)),
        ],
        compiler_params=pltpu.CompilerParams(
            collective_id=0, has_side_effects=True, vmem_limit_bytes=56 << 20
        ),
        name="decode",
    )(
        live_frames,
        plan_owner.reshape(1, rows),
        plan_slot.reshape(1, rows),
        seq_rows,
        norm_gain.reshape(1, channels),
        norm_bias.reshape(1, channels),
        conv_bias.reshape(1, out_width),
        conv_weight.transpose(0, 1, 3, 2, 4).reshape(9, 3 * channels, out_width),
    )
    return decoded.reshape(1, 1, LT, TH, TW, out_width)


def solution(mesh):
    return jax.shard_map(
        on_device,
        mesh=mesh,
        in_specs=(
            P(("tile", "clip"), None),
            P(("tile", "clip")),
            P(("tile", "clip")),
            P(),
            P(),
            P(),
            P(),
            P(),
        ),
        out_specs=P("clip", "tile", None, None, None, None),
        check_vma=False,
    )
```
